32 devices in a mesh: ctx: 8 (over y, x, core), qry: 4 (over z).
Axes of the slice: x: 2, y: 2, z: 4, core: 2. Of those that a mesh axis runs over, the one named last changes fastest.
Arguments:
- idx_query: bfloat16 [32, 8192], P('ctx', 'qry'), may hold values from -200 to 200
- idx_weight: bfloat16 [32, 64], P('ctx', 'qry'), may hold values from -3 to 3
- idx_keys: bfloat16 [16384, 128], P('ctx'), may hold values from -6 to 6
- q_latent: bfloat16 [32, 73728], P(('ctx', 'qry')), may hold values from -400 to 400
- latent_cache: bfloat16 [16384, 576], P('ctx'), may hold values from -20 to 20
- page_ids: int32 [32, 32], P(('ctx', 'qry')), may hold values from 0 to 255, as said below
Outputs:
- index_logp: float32 [32, 16384], P(('ctx', 'qry'))
- latent_out: bfloat16 [32, 65536], P(('ctx', 'qry'))
The draws below stay inside these ranges and needn't reach their ends.
Inputs may be any that keep to these rules, and one draw needn't show every extreme that they name: `page_ids`: each row names 32 distinct pages, and no page id appears twice in the 1 row of one device (aligned blocks of 1 row). Page p holds tokens p * 64 to p * 64 + 63; ctx index j holds pages j * 32 to (j + 1) * 32 - 1. Of the 32 ids in the rows of one device, at most 8 lie on one ctx index, and in every such block some ctx index holds exactly 8.
All inputs are finite; a program needn't handle non-finite values.
Results may differ from the reference program's by a relative error of at most 0.013.
Values may be sent and summed in bfloat16 or wider, within the bound.
A program may use at most 64 MiB of HBM per device.

```python
import math
import jax
import jax.numpy as jnp
from jax import lax

H_IDX = 64
D_IDX = 128
H = 128
D_LAT = 512
D_ROPE = 64
QK_NOPE = 128
DK = 576
PAGE = 64
TOPP = 32
CTX_DEV = 2048
QR_DEV = 1
MOST = 8
PAGES_DEV = 32
PAGES = 256
CTX = 16384
QROWS = 32


def draw_idx_query(key, part):
    norm_key = jax.random.fold_in(jax.random.fold_in(key, 11), 0)
    values = jnp.clip(jax.random.normal(norm_key, (QROWS, H_IDX * D_IDX), jnp.float32), -6.0, 6.0)
    return jnp.clip(values, -200.0, 200.0).astype(jnp.bfloat16)


def draw_idx_keys(key, part):
    norm_key = jax.random.fold_in(jax.random.fold_in(key, 13), 0)
    values = jnp.clip(jax.random.normal(norm_key, (CTX, D_IDX), jnp.float32), -6.0, 6.0) / math.sqrt(D_IDX)
    return jnp.clip(values, -6.0, 6.0).astype(jnp.bfloat16)


def draw_q_latent(key, part):
    norm_key = jax.random.fold_in(jax.random.fold_in(key, 17), 0)
    values = jnp.clip(jax.random.normal(norm_key, (QROWS, H, DK), jnp.float32), -6.0, 6.0)
    return jnp.clip(values, -400.0, 400.0).reshape(QROWS, H * DK).astype(jnp.bfloat16)


def draw_latent_cache(key, part):
    norm_key = jax.random.fold_in(jax.random.fold_in(key, 19), 0)
    values = jnp.clip(jax.random.normal(norm_key, (CTX, DK), jnp.float32), -6.0, 6.0)
    return jnp.clip(values, -20.0, 20.0).astype(jnp.bfloat16)


def draw_page_ids(key, part):
    shard_count = PAGES // PAGES_DEV
    wanted = QR_DEV * TOPP
    couple_count = shard_count * MOST
    heat_key, block_key = jax.random.split(jax.random.fold_in(key, 23))
    partition_load = jax.random.randint(heat_key, (shard_count,), 0, 4)
    couple_holder = jnp.arange(couple_count, dtype=jnp.int32) // MOST
    pair_copy = jnp.arange(couple_count, dtype=jnp.int32) % MOST

    def one_block(block_seed):
        seeds = jax.random.split(block_seed, 4)
        random_noise = jax.random.randint(seeds[0], (couple_count,), 0, 65536)
        compelled_pick = jax.random.randint(seeds[1], (), 0, shard_count)
        compelled_reward = jnp.where(couple_holder == compelled_pick, 1048576, 0)
        couple_score = (random_noise + partition_load[couple_holder] * 32768 + compelled_reward) * couple_count + jnp.arange(couple_count, dtype=jnp.int32)
        picked = lax.top_k(couple_score, wanted)[1]
        offset = jax.random.randint(seeds[2], (shard_count,), 0, PAGES_DEV)
        owner_shard = couple_holder[picked]
        local_page = (offset[owner_shard] + pair_copy[picked]) % PAGES_DEV
        page_list = owner_shard * PAGES_DEV + local_page
        shuffled = jax.random.permutation(seeds[3], page_list)
        return shuffled.reshape(QR_DEV, TOPP)
    block_seeds = jax.random.split(block_key, QROWS // QR_DEV)
    return jax.vmap(one_block)(block_seeds).reshape(QROWS, TOPP).astype(jnp.int32)


def block_scale(rng, dims, cuts, low, high):
    level, own = 1.0, jax.random.fold_in(rng, 6)
    for position, blocks in cuts:
        heights = jnp.exp(jax.random.uniform(jax.random.fold_in(own, position), (blocks,), jnp.float32, low / len(cuts), high / len(cuts)))
        level = level * jnp.repeat(heights, dims[position] // blocks).reshape([-1 if axis == position else 1 for axis in range(len(dims))])
    return level


def normal_values(key, dims, scale, most, cuts=(), kind=jnp.bfloat16):
    gain = block_scale(key, dims, cuts, -0.22, 0.18) if cuts else 1.0
    values = jax.random.normal(key, dims, jnp.float32) * scale * gain
    return jnp.minimum(jnp.maximum(values, -most), most).astype(kind)


def setup_inputs(seed: int = 0) -> dict:
    key_of = jax.random.split(jax.random.key(seed), 7)
    idx_query = draw_idx_query(jax.random.fold_in(key_of[6], 71), 0)
    idx_weight = normal_values(key_of[1], (QROWS, H_IDX), 0.7, 3.0, ((0, 8), (1, 4)))
    idx_keys = draw_idx_keys(jax.random.fold_in(key_of[6], 71), 0)
    q_latent = draw_q_latent(jax.random.fold_in(key_of[6], 71), 0)
    latent_cache = draw_latent_cache(jax.random.fold_in(key_of[6], 71), 0)
    page_ids = draw_page_ids(jax.random.fold_in(key_of[6], 71), 0)
    return dict(idx_query=idx_query, idx_weight=idx_weight, idx_keys=idx_keys, q_latent=q_latent, latent_cache=latent_cache, page_ids=page_ids)


def reference(idx_query, idx_weight, idx_keys, q_latent, latent_cache, page_ids):
    block_width = min(512, CTX_DEV)
    query_flat = idx_query.astype(jnp.float32).reshape(QROWS * H_IDX, D_IDX)
    head_weights = idx_weight.astype(jnp.float32)
    key_blocks = idx_keys.astype(jnp.float32).reshape(CTX // block_width, block_width, D_IDX)

    def index_block(key_block):
        head_dots = jnp.dot(query_flat, key_block.T)
        active = jnp.maximum(head_dots, 0.0).reshape(QROWS, H_IDX, block_width)
        return jnp.sum(active * head_weights[:, :, None], axis=1)

    blocks = lax.map(index_block, key_blocks)
    scores = jnp.moveaxis(blocks, 0, 1).reshape(QROWS, CTX)
    row_max = jnp.max(scores, axis=1, keepdims=True)
    row_total = jnp.sum(jnp.exp(scores - row_max), axis=1, keepdims=True)
    index_logp = scores - (row_max + jnp.log(row_total)) + jnp.log(CTX * 1.0)

    page_store = latent_cache.reshape(PAGES, PAGE, DK)
    logit_scale = (QK_NOPE + D_ROPE) ** -0.5

    def attend(pair):
        query_row, row_pages = pair
        key_rows = page_store[row_pages].reshape(TOPP * PAGE, DK)
        logits = jnp.dot(query_row.reshape(H, DK).astype(jnp.float32), key_rows.astype(jnp.float32).T) * logit_scale
        logit_max = jnp.max(logits, axis=1, keepdims=True)
        expo = jnp.exp(logits - logit_max)
        att_weights = (expo / jnp.sum(expo, axis=1, keepdims=True)).astype(jnp.bfloat16)
        mixed_rows = jnp.dot(att_weights, key_rows[:, :D_LAT], preferred_element_type=jnp.float32)
        return mixed_rows.astype(jnp.bfloat16).reshape(H * D_LAT)

    latent_out = lax.map(attend, (q_latent, page_ids))
    return index_logp, latent_out
```

```python
import functools

import jax
import jax.numpy as jnp
from jax import lax
from jax.experimental import pallas as pl
from jax.experimental.pallas import tpu as pltpu
from jax.sharding import PartitionSpec as P

H_IDX = 64
D_IDX = 128
H = 128
D_LAT = 512
D_ROPE = 64
QK_NOPE = 128
PAGE = 64

MESH = pl.DeviceIdType.MESH
LOG2E = 1.4426950408889634
NEG = -1e30


def flip(a, r, n):
    out, bit = 0, 1
    while bit < n:
        x, y = (a // bit) % 2, (r // bit) % 2
        out = out + bit * (x + y - 2 * x * y)
        bit *= 2
    return out


def repeat(lo, hi, body):
    if hi - lo <= 8:
        for i in range(lo, hi):
            body(i)
    else:

        def step(i, carry):
            body(i)
            return carry

        lax.fori_loop(lo, hi, step, 0)


def kernel(
    n, g, group, chunk, ichunk,
    mine_ref, cache_ref, keys_ref, query_ref,
    logp_ref, out_ref,
    zed, idx, kt, qr, logits, acc, osend, orecv, tsend, trecv, ssend, srecv,
    z_s, z_r, i_s, i_r, k_s, k_r, q_s, q_r, o_s, o_r, t_s, t_r, s_s, s_r, loc,
):
    c = lax.axis_index("ctx")
    z = lax.axis_index("qry")
    core = c % 2
    ctx_dev = keys_ref.shape[0]
    width = cache_ref.shape[0]
    half = H // 2
    hb = mine_ref.shape[2]

    barrier = pltpu.get_barrier_semaphore()

    def greet_z(r):
        pl.semaphore_signal(
            barrier, inc=1, device_id=(c, flip(z, r, g)), device_id_type=MESH
        )

    def greet_c(r):
        pl.semaphore_signal(
            barrier, inc=1, device_id=(flip(c, r, n), z), device_id_type=MESH
        )

    repeat(1, g, greet_z)
    repeat(1, n, greet_c)

    own_z = pltpu.make_async_copy(mine_ref.at[z], zed.at[z], loc.at[0])
    own_k = pltpu.make_async_copy(
        cache_ref, kt.at[core, pl.ds(0, width), :], loc.at[1]
    )
    own_q = pltpu.make_async_copy(query_ref.at[c // 2, core], qr.at[0], loc.at[2])
    own_z.start()
    own_k.start()
    own_q.start()

    def z_copy(r):
        peer = flip(z, r, g)
        return pltpu.make_async_remote_copy(
            src_ref=mine_ref.at[peer], dst_ref=zed.at[z],
            send_sem=z_s.at[r], recv_sem=z_r.at[r],
            device_id=(c, peer), device_id_type=MESH,
        )

    def k_copy():
        return pltpu.make_async_remote_copy(
            src_ref=cache_ref, dst_ref=kt.at[core, pl.ds(0, width), :],
            send_sem=k_s, recv_sem=k_r,
            device_id=(flip(c, 1, n), z), device_id_type=MESH,
        )

    def c_copy(src, dst, send, recv, r):
        return pltpu.make_async_remote_copy(
            src_ref=src, dst_ref=dst, send_sem=send.at[r], recv_sem=recv.at[r],
            device_id=(flip(c, r, n), z), device_id_type=MESH,
        )

    def q_copy(r):
        peer = flip(c, r, n)
        return c_copy(query_ref.at[peer // 2, peer % 2], qr.at[r], q_s, q_r, r)

    def i_copy(r):
        return c_copy(zed, idx.at[r], i_s, i_r, r)

    def o_copy(r):
        return c_copy(osend.at[r], orecv.at[r], o_s, o_r, r)

    def t_copy(r):
        return c_copy(tsend.at[r], trecv.at[r], t_s, t_r, r)

    def s_copy(r):
        return c_copy(ssend.at[r], srecv.at[c], s_s, s_r, r)

    pages_dev = ctx_dev // PAGE
    page_row = lax.broadcasted_iota(jnp.int32, (2 * pages_dev, ctx_dev), 0)
    page_col = lax.broadcasted_iota(jnp.int32, (2 * pages_dev, ctx_dev), 1) // PAGE
    for h in range(2):
        kt[h, width:, :] = jnp.where(page_row == page_col + h * pages_dev, 1.0, 0.0).astype(
            jnp.bfloat16
        )

    pl.semaphore_wait(barrier, (g - 1) + (n - 1))

    repeat(1, g, lambda r: z_copy(r).start())
    k_copy().start()
    first = max(2, n * 3 // 4)
    repeat(1, first, lambda r: q_copy(r).start())
    own_z.wait()
    repeat(1, g, lambda r: z_copy(r).wait_recv())
    own_i = pltpu.make_async_copy(zed, idx.at[0], loc.at[3])
    own_i.start()
    repeat(1, n, lambda r: i_copy(r).start())
    repeat(first, n, lambda r: q_copy(r).start())

    own_i.wait()
    repeat(1, n, lambda r: i_copy(r).wait_recv())

    def index_rows(r):
        rows = idx[r]
        q_rows = rows[:, 0].reshape(g * hb, D_IDX)
        w_rows = rows[:, 1].reshape(g * hb, D_IDX).astype(jnp.float32)
        w_wide = jnp.concatenate([w_rows] * (ichunk // D_IDX), axis=1)

        def block(s, carry):
            at = pl.ds(pl.multiple_of(s * ichunk, ichunk), ichunk)
            dots = lax.dot_general(
                q_rows, keys_ref[at, :], (((1,), (1,)), ((), ())),
                preferred_element_type=jnp.float32,
            )
            ssend[r, :, at] = jnp.sum(jnp.maximum(dots, 0.0) * w_wide, axis=0, keepdims=True)
            return carry

        lax.fori_loop(0, ctx_dev // ichunk, block, 0)

    repeat(0, n, index_rows)
    repeat(1, n, lambda r: s_copy(r).start())
    own_s = pltpu.make_async_copy(ssend.at[0], srecv.at[c], loc.at[4])
    own_s.start()

    own_k.wait()
    own_q.wait()
    k_copy().wait_recv()
    per = ctx_dev // chunk
    scale = ((QK_NOPE + D_ROPE) ** -0.5) * LOG2E
    m_rows = group * half

    def rows_of(b):
        for j in range(group):
            r = b * group + j
            if isinstance(r, int):
                if r > 0:
                    q_copy(r).wait_recv()
            else:

                @pl.when(r > 0)
                def _():
                    q_copy(r).wait_recv()

        def part_one(s, peak):
            keys = pl.ds(pl.multiple_of((s % per) * chunk, chunk), chunk)
            dots = jnp.dot(
                qr[pl.ds(b * group, group)].reshape(m_rows, qr.shape[2]),
                kt[s // per, :, keys],
                preferred_element_type=jnp.float32,
            ) * scale
            logits[s] = dots
            for t in range(chunk // 128):
                peak = jnp.maximum(peak, dots[:, t * 128 : (t + 1) * 128])
            return peak

        peak = lax.fori_loop(
            0, 2 * per, part_one, jnp.full((m_rows, 128), -jnp.inf, jnp.float32)
        )
        top = jnp.max(peak, axis=1, keepdims=True)
        acc[...] = jnp.zeros_like(acc)

        def part_two(s, total):
            keys = pl.ds(pl.multiple_of((s % per) * chunk, chunk), chunk)
            expo = jnp.exp2(logits[s] - top)
            for t in range(chunk // 128):
                total = total + expo[:, t * 128 : (t + 1) * 128]
            acc[...] += lax.dot_general(
                expo.astype(jnp.bfloat16), kt[s // per, :D_LAT, keys],
                (((1,), (1,)), ((), ())), preferred_element_type=jnp.float32,
            )
            return total

        total = lax.fori_loop(0, 2 * per, part_two, jnp.zeros((m_rows, 128), jnp.float32))
        mass = jnp.sum(total, axis=1, keepdims=True)
        lane = lax.broadcasted_iota(jnp.int32, (m_rows, 128), 1)
        stats = jnp.where(lane == 0, top, mass)
        osend[pl.ds(b * group, group)] = acc[...].astype(jnp.bfloat16).reshape(
            group, half, D_LAT
        )
        for j in range(group):
            turned = jnp.transpose(stats[j * half : (j + 1) * half, :])
            tsend[b * group + j] = jnp.concatenate([turned[:8], turned[:8]], axis=1)
        for j in range(group):
            r = b * group + j
            if isinstance(r, int):
                if r > 0:
                    t_copy(r).start()
                    o_copy(r).start()
            else:

                @pl.when(r > 0)
                def _():
                    t_copy(r).start()
                    o_copy(r).start()

    repeat(0, n // group, rows_of)

    own_s.wait()

    def take_scores(r):
        peer = flip(c, r, n)
        c_copy(ssend.at[r], srecv.at[peer], s_s, s_r, r).wait_recv()

    repeat(1, n, take_scores)
    table = srecv[...]
    row_max = jnp.max(table)
    row_total = jnp.sum(jnp.exp(table - row_max), keepdims=True)
    logp_ref[...] = table - (row_max + jnp.log(row_total)) + jnp.log(
        jnp.full((1, 1, 1), n * ctx_dev, jnp.float32)
    )

    def arrive(r):
        t_copy(r).wait_recv()
        o_copy(r).wait_recv()

    repeat(1, n, arrive)
    for parity in range(2):
        tops, masses = [], []
        for r in range(parity, n, 2):
            stat = tsend[r] if r == 0 else trecv[r]
            col = jnp.transpose(stat)[:half]
            tops.append(col[:, 0:1])
            masses.append(col[:, 1:2])
        best = functools.reduce(jnp.maximum, tops)
        weights = [jnp.exp2(t - best) for t in tops]
        mass = functools.reduce(jnp.add, [w * l for w, l in zip(weights, masses)])
        mixed = jnp.zeros((half, D_LAT), jnp.float32)
        for s, r in enumerate(range(parity, n, 2)):
            value = osend[r] if r == 0 else orecv[r]
            mixed = mixed + value.astype(jnp.float32) * (weights[s] / mass)
        out_ref[(core + parity) % 2] = mixed.astype(jnp.bfloat16)

    repeat(1, g, lambda r: z_copy(r).wait_send())
    k_copy().wait_send()

    def sent(r):
        q_copy(r).wait_send()
        i_copy(r).wait_send()
        o_copy(r).wait_send()
        t_copy(r).wait_send()
        s_copy(r).wait_send()

    repeat(1, n, sent)


def per_device(n, g, idx_query, idx_weight, idx_keys, q_latent, latent_cache, page_ids):
    hb = H_IDX // g
    ctx_dev, width = idx_keys.shape[0], latent_cache.shape[1]
    pages_dev = ctx_dev // PAGE
    chips = n // 2
    group, chunk, ichunk = 4, 512, 512

    heads = idx_query.reshape(g, 1, hb, D_IDX)
    gains = jnp.broadcast_to(idx_weight.reshape(g, 1, hb, 1), heads.shape)
    mine = jnp.concatenate([heads, gains], axis=1)
    chip_pages = jnp.arange(n * pages_dev, dtype=jnp.int32)
    hit = jnp.any(page_ids.reshape(-1, 1) == chip_pages[None, :], axis=0)
    flags = jnp.where(hit, 0.0, NEG).astype(jnp.bfloat16).reshape(chips, 1, 2 * pages_dev)
    query = jnp.concatenate(
        [
            jnp.broadcast_to(q_latent.reshape(1, H, width), (chips, H, width)),
            jnp.broadcast_to(flags, (chips, H, 2 * pages_dev)),
        ],
        axis=2,
    ).reshape(chips, 2, H // 2, width + 2 * pages_dev)

    full = width + 2 * pages_dev
    half = H // 2
    dma = pltpu.SemaphoreType.DMA
    vmem = pl.BlockSpec(memory_space=pltpu.VMEM)
    logp, out = pl.pallas_call(
        functools.partial(kernel, n, g, group, chunk, ichunk),
        out_shape=(
            jax.ShapeDtypeStruct((n, 1, ctx_dev), jnp.float32),
            jax.ShapeDtypeStruct((2, half, D_LAT), jnp.bfloat16),
        ),
        in_specs=[vmem, pl.BlockSpec(memory_space=pl.ANY), vmem, vmem],
        out_specs=(vmem, vmem),
        scratch_shapes=[
            pltpu.VMEM((g, 2, hb, D_IDX), jnp.bfloat16),
            pltpu.VMEM((n, g, 2, hb, D_IDX), jnp.bfloat16),
            pltpu.VMEM((2, full, ctx_dev), jnp.bfloat16),
            pltpu.VMEM((n, half, full), jnp.bfloat16),
            pltpu.VMEM((2 * ctx_dev // chunk, group * half, chunk), jnp.float32),
            pltpu.VMEM((group * half, D_LAT), jnp.float32),
            pltpu.VMEM((n, half, D_LAT), jnp.bfloat16),
            pltpu.VMEM((n, half, D_LAT), jnp.bfloat16),
            pltpu.VMEM((n, 8, 128), jnp.float32),
            pltpu.VMEM((n, 8, 128), jnp.float32),
            pltpu.VMEM((n, 1, ctx_dev), jnp.float32),
            pltpu.VMEM((n, 1, ctx_dev), jnp.float32),
            dma((g,)), dma((g,)),
            dma((n,)), dma((n,)),
            dma, dma,
            dma((n,)), dma((n,)),
            dma((n,)), dma((n,)),
            dma((n,)), dma((n,)),
            dma((n,)), dma((n,)),
            dma((5,)),
        ],
        compiler_params=pltpu.CompilerParams(
            collective_id=0, has_side_effects=True, vmem_limit_bytes=60 * 1024 * 1024
        ),
    )(mine, latent_cache.T, idx_keys, query)
    return logp.reshape(1, n * ctx_dev), out.reshape(1, H * D_LAT)


def solution(mesh):
    in_specs = (
        P("ctx", "qry"),
        P("ctx", "qry"),
        P("ctx", None),
        P(("ctx", "qry"), None),
        P("ctx", None),
        P(("ctx", "qry"), None),
    )
    out_specs = (P(("ctx", "qry"), None), P(("ctx", "qry"), None))
    return jax.shard_map(
        functools.partial(per_device, mesh.shape["ctx"], mesh.shape["qry"]),
        mesh=mesh, in_specs=in_specs, out_specs=out_specs, check_vma=False,
    )
```

```python
import functools

import jax
import jax.numpy as jnp
from jax import lax
from jax.experimental import pallas as pl
from jax.experimental.pallas import tpu as pltpu
from jax.sharding import PartitionSpec as P

H_IDX = 64
D_IDX = 128
H = 128
D_LAT = 512
D_ROPE = 64
QK_NOPE = 128
PAGE = 64

MESH = pl.DeviceIdType.MESH
LOG2E = 1.4426950408889634
NEG = -1e30


def flip(a, r, n):
    out, bit = 0, 1
    while bit < n:
        x, y = (a // bit) % 2, (r // bit) % 2
        out = out + bit * (x + y - 2 * x * y)
        bit *= 2
    return out


def repeat(lo, hi, body):
    if hi - lo <= 8:
        for i in range(lo, hi):
            body(i)
    else:

        def step(i, carry):
            body(i)
            return carry

        lax.fori_loop(lo, hi, step, 0)


def kernel(
    n, g, group, chunk, ichunk, unroll,
    heads_ref, gains_ref, cache_ref, keys_ref, latent_ref, pages_ref,
    logp_ref, out_ref,
    head_rows, mine_ref, pairs, query_ref, flat_query, wide_gains,
    zed, idx, kt, qr, logits, acc, osend, orecv, tsend, trecv, ssend, srecv,
    z_s, z_r, i_s, i_r, k_s, k_r, q_s, q_r, o_s, o_r, t_s, t_r, s_s, s_r, loc,
):
    c = lax.axis_index("ctx")
    z = lax.axis_index("qry")
    core = c % 2
    ctx_dev = keys_ref.shape[0]
    width = cache_ref.shape[0]
    half = H // 2
    hb = mine_ref.shape[2]

    barrier = pltpu.get_barrier_semaphore()

    def greet_z(r):
        pl.semaphore_signal(
            barrier, inc=1, device_id=(c, flip(z, r, g)), device_id_type=MESH
        )

    def greet_c(r):
        pl.semaphore_signal(
            barrier, inc=1, device_id=(flip(c, r, n), z), device_id_type=MESH
        )

    repeat(1, g, greet_z)
    repeat(1, n, greet_c)

    own_k = pltpu.make_async_copy(
        cache_ref, kt.at[core, pl.ds(0, width), :], loc.at[1]
    )
    own_k.start()

    for h in range(hb):
        piece = heads_ref[:, h * D_IDX : (h + 1) * D_IDX].astype(jnp.float32)
        for r in range(g):
            head_rows[r, h : h + 1, :] = piece[r : r + 1]
    eye = lax.broadcasted_iota(jnp.int32, (hb, hb), 0) == lax.broadcasted_iota(
        jnp.int32, (hb, hb), 1
    )
    gains = gains_ref[...].astype(jnp.float32)
    for r in range(g):
        mine_ref[r, 0] = head_rows[r].astype(jnp.bfloat16)
        gain = jnp.sum(jnp.where(eye, gains[r : r + 1], 0.0), axis=1, keepdims=True)
        mine_ref[r, 1] = jnp.broadcast_to(gain, (hb, D_IDX)).astype(jnp.bfloat16)

    full = query_ref.shape[3]
    for p in range(half):
        pairs[p : p + 1, :] = latent_ref[:, p * 2 * width : (p + 1) * 2 * width].astype(
            jnp.float32
        )
    topp = pages_ref.shape[1]
    eye = lax.broadcasted_iota(jnp.int32, (topp, topp), 0) == lax.broadcasted_iota(
        jnp.int32, (topp, topp), 1
    )
    ids = jnp.sum(
        jnp.where(eye, pages_ref[...].astype(jnp.float32), 0.0), axis=1, keepdims=True
    )
    spare = 2 * (ctx_dev // PAGE)
    lane = lax.broadcasted_iota(jnp.int32, (topp, 128), 1)
    tail_lane = lax.broadcasted_iota(jnp.int32, (half, 128), 1)
    even = pairs[:, :full]
    odd = pltpu.roll(pairs[:, 2 * width - full :], width, 1)
    for j in range(n // 2):
        page = (lane - (128 - spare) + j * spare).astype(jnp.float32)
        hit = jnp.max(jnp.where(ids == page, 1.0, 0.0), axis=0, keepdims=True)
        flags = jnp.where(hit > 0.5, 0.0, NEG)
        for h, rows in enumerate((even, odd)):
            query_ref[j, h, :, : full - 128] = rows[:, : full - 128].astype(jnp.bfloat16)
            query_ref[j, h, :, full - 128 :] = jnp.where(
                tail_lane < 128 - spare, rows[:, full - 128 :], flags
            ).astype(jnp.bfloat16)

    def z_copy(r):
        peer = flip(z, r, g)
        return pltpu.make_async_remote_copy(
            src_ref=mine_ref.at[peer], dst_ref=zed.at[z],
            send_sem=z_s.at[r], recv_sem=z_r.at[r],
            device_id=(c, peer), device_id_type=MESH,
        )

    def k_copy():
        return pltpu.make_async_remote_copy(
            src_ref=cache_ref, dst_ref=kt.at[core, pl.ds(0, width), :],
            send_sem=k_s, recv_sem=k_r,
            device_id=(flip(c, 1, n), z), device_id_type=MESH,
        )

    def c_copy(src, dst, send, recv, r):
        return pltpu.make_async_remote_copy(
            src_ref=src, dst_ref=dst, send_sem=send.at[r], recv_sem=recv.at[r],
            device_id=(flip(c, r, n), z), device_id_type=MESH,
        )

    def q_copy(r):
        peer = flip(c, r, n)
        return c_copy(query_ref.at[peer // 2, peer % 2], qr.at[r], q_s, q_r, r)

    def i_copy(r):
        return c_copy(zed, idx.at[r], i_s, i_r, r)

    def o_copy(r):
        return c_copy(osend.at[r], orecv.at[r], o_s, o_r, r)

    def t_copy(r):
        return c_copy(tsend.at[r], trecv.at[r], t_s, t_r, r)

    def s_copy(r):
        return c_copy(ssend.at[r], srecv.at[c], s_s, s_r, r)

    pages_dev = ctx_dev // PAGE
    page_row = lax.broadcasted_iota(jnp.int32, (2 * pages_dev, ctx_dev), 0)
    page_col = lax.broadcasted_iota(jnp.int32, (2 * pages_dev, ctx_dev), 1) // PAGE
    for h in range(2):
        kt[h, width:, :] = jnp.where(page_row == page_col + h * pages_dev, 1.0, 0.0).astype(
            jnp.bfloat16
        )

    pl.semaphore_wait(barrier, (g - 1) + (n - 1))

    own_z = pltpu.make_async_copy(mine_ref.at[z], zed.at[z], loc.at[0])
    own_q = pltpu.make_async_copy(query_ref.at[c // 2, core], qr.at[0], loc.at[2])
    own_z.start()
    own_q.start()
    repeat(1, g, lambda r: z_copy(r).start())
    k_copy().start()
    first = max(2, n * 3 // 4)
    repeat(1, first, lambda r: q_copy(r).start())
    own_z.wait()
    repeat(1, g, lambda r: z_copy(r).wait_recv())
    own_i = pltpu.make_async_copy(zed, idx.at[0], loc.at[3])
    own_i.start()
    repeat(1, n, lambda r: i_copy(r).start())
    repeat(first, n, lambda r: q_copy(r).start())

    def index_rows():
        own_i.wait()
        repeat(1, n, lambda r: i_copy(r).wait_recv())
        count = g * hb

        def lay(r):
            rows = idx[r]
            flat_query[r] = rows[:, 0].reshape(count, D_IDX)
            wide_gains[r] = rows[:, 1].reshape(count, D_IDX).astype(jnp.float32)

        repeat(0, n, lay)

        def block(s, carry):
            at = pl.ds(pl.multiple_of(s * ichunk, ichunk), ichunk)
            keys = keys_ref[at, :]
            for b in range(n // 4):
                dots = lax.dot_general(
                    flat_query[4 * b : 4 * b + 4].reshape(4 * count, D_IDX), keys,
                    (((1,), (1,)), ((), ())), preferred_element_type=jnp.float32,
                )
                for j in range(4):
                    r = 4 * b + j
                    gain = wide_gains[r]
                    sums = [
                        jnp.sum(
                            jnp.maximum(
                                dots[j * count : (j + 1) * count, t * 128 : (t + 1) * 128], 0.0
                            ) * gain,
                            axis=0, keepdims=True,
                        )
                        for t in range(ichunk // 128)
                    ]
                    ssend[r, :, at] = jnp.concatenate(sums, axis=1)
            return carry

        lax.fori_loop(0, ctx_dev // ichunk, block, 0)
        repeat(1, n, lambda r: s_copy(r).start())

    own_s = pltpu.make_async_copy(ssend.at[0], srecv.at[c], loc.at[4])

    own_k.wait()
    own_q.wait()
    k_copy().wait_recv()
    per = ctx_dev // chunk
    scale = ((QK_NOPE + D_ROPE) ** -0.5) * LOG2E
    m_rows = group * half

    def rows_of(b):
        for j in range(group):
            r = b * group + j
            if isinstance(r, int):
                if r > 0:
                    q_copy(r).wait_recv()
            else:

                @pl.when(r > 0)
                def _():
                    q_copy(r).wait_recv()

        def part_one(s, peak):
            keys = pl.ds(pl.multiple_of((s % per) * chunk, chunk), chunk)
            dots = jnp.dot(
                qr[pl.ds(b * group, group)].reshape(m_rows, qr.shape[2]),
                kt[s // per, :, keys],
                preferred_element_type=jnp.float32,
            ) * scale
            logits[s] = dots
            for t in range(chunk // 128):
                peak = jnp.maximum(peak, dots[:, t * 128 : (t + 1) * 128])
            return peak

        peak = lax.fori_loop(
            0, 2 * per, part_one, jnp.full((m_rows, 128), -jnp.inf, jnp.float32), unroll=unroll
        )
        top = jnp.max(peak, axis=1, keepdims=True)
        acc[...] = jnp.zeros_like(acc)

        def part_two(s, total):
            keys = pl.ds(pl.multiple_of((s % per) * chunk, chunk), chunk)
            expo = jnp.exp2(logits[s] - top)
            for t in range(chunk // 128):
                total = total + expo[:, t * 128 : (t + 1) * 128]
            acc[...] += lax.dot_general(
                expo.astype(jnp.bfloat16), kt[s // per, :D_LAT, keys],
                (((1,), (1,)), ((), ())), preferred_element_type=jnp.float32,
            )
            return total

        total = lax.fori_loop(0, 2 * per, part_two, jnp.zeros((m_rows, 128), jnp.float32), unroll=unroll)
        mass = jnp.sum(total, axis=1, keepdims=True)
        lane = lax.broadcasted_iota(jnp.int32, (m_rows, 128), 1)
        stats = jnp.where(lane == 0, top, mass)
        osend[pl.ds(b * group, group)] = acc[...].astype(jnp.bfloat16).reshape(
            group, half, D_LAT
        )
        for j in range(group):
            turned = jnp.transpose(stats[j * half : (j + 1) * half, :])
            tsend[b * group + j] = jnp.concatenate([turned[:8], turned[:8]], axis=1)
        for j in range(group):
            r = b * group + j
            if isinstance(r, int):
                if r > 0:
                    t_copy(r).start()
                    o_copy(r).start()
            else:

                @pl.when(r > 0)
                def _():
                    t_copy(r).start()
                    o_copy(r).start()

    rows_of(0)
    index_rows()
    own_s.start()
    repeat(1, n // group, rows_of)

    own_s.wait()

    def take_scores(r):
        peer = flip(c, r, n)
        c_copy(ssend.at[r], srecv.at[peer], s_s, s_r, r).wait_recv()

    repeat(1, n, take_scores)
    table = srecv[...]
    row_max = jnp.max(table)
    row_total = jnp.sum(jnp.exp(table - row_max), keepdims=True)
    logp_ref[...] = table - (row_max + jnp.log(row_total)) + jnp.log(
        jnp.full((1, 1, 1), n * ctx_dev, jnp.float32)
    )

    def arrive(r):
        t_copy(r).wait_recv()
        o_copy(r).wait_recv()

    repeat(1, n, arrive)
    mixes = []
    for parity in range(2):
        tops, masses = [], []
        for r in range(parity, n, 2):
            stat = tsend[r] if r == 0 else trecv[r]
            col = jnp.transpose(stat)[:half]
            tops.append(col[:, 0:1])
            masses.append(col[:, 1:2])
        best = functools.reduce(jnp.maximum, tops)
        weights = [jnp.exp2(t - best) for t in tops]
        mass = functools.reduce(jnp.add, [w * l for w, l in zip(weights, masses)])
        mixed = jnp.zeros((half, D_LAT), jnp.float32)
        for s, r in enumerate(range(parity, n, 2)):
            value = osend[r] if r == 0 else orecv[r]
            mixed = mixed + value.astype(jnp.float32) * (weights[s] / mass)
        mixes.append(mixed)

    for h in range(2):
        out_ref[:, h * D_LAT : (h + 1) * D_LAT] = jnp.where(
            core == h, mixes[0], mixes[1]
        ).astype(jnp.bfloat16)

    repeat(1, g, lambda r: z_copy(r).wait_send())
    k_copy().wait_send()

    def sent(r):
        q_copy(r).wait_send()
        i_copy(r).wait_send()
        o_copy(r).wait_send()
        t_copy(r).wait_send()
        s_copy(r).wait_send()

    repeat(1, n, sent)


def per_device(n, g, idx_query, idx_weight, idx_keys, q_latent, latent_cache, page_ids):
    hb = H_IDX // g
    ctx_dev, width = idx_keys.shape[0], latent_cache.shape[1]
    pages_dev = ctx_dev // PAGE
    chips = n // 2
    group, chunk, ichunk, unroll = 4, 1024, 256, True
    full = width + 2 * pages_dev
    half = H // 2
    dma = pltpu.SemaphoreType.DMA
    vmem = pl.BlockSpec(memory_space=pltpu.VMEM)
    logp, out = pl.pallas_call(
        functools.partial(kernel, n, g, group, chunk, ichunk, unroll),
        out_shape=(
            jax.ShapeDtypeStruct((n, 1, ctx_dev), jnp.float32),
            jax.ShapeDtypeStruct((half, 2 * D_LAT), jnp.bfloat16),
        ),
        in_specs=[vmem, vmem, pl.BlockSpec(memory_space=pl.ANY), vmem, vmem, vmem],
        out_specs=(vmem, vmem),
        scratch_shapes=[
            pltpu.VMEM((g, hb, D_IDX), jnp.float32),
            pltpu.VMEM((g, 2, hb, D_IDX), jnp.bfloat16),
            pltpu.VMEM((half, 2 * width), jnp.float32),
            pltpu.VMEM((chips, 2, half, full), jnp.bfloat16),
            pltpu.VMEM((n, g * hb, D_IDX), jnp.bfloat16),
            pltpu.VMEM((n, g * hb, D_IDX), jnp.float32),
            pltpu.VMEM((g, 2, hb, D_IDX), jnp.bfloat16),
            pltpu.VMEM((n, g, 2, hb, D_IDX), jnp.bfloat16),
            pltpu.VMEM((2, full, ctx_dev), jnp.bfloat16),
            pltpu.VMEM((n, half, full), jnp.bfloat16),
            pltpu.VMEM((2 * ctx_dev // chunk, group * half, chunk), jnp.float32),
            pltpu.VMEM((group * half, D_LAT), jnp.float32),
            pltpu.VMEM((n, half, D_LAT), jnp.bfloat16),
            pltpu.VMEM((n, half, D_LAT), jnp.bfloat16),
            pltpu.VMEM((n, 8, 128), jnp.float32),
            pltpu.VMEM((n, 8, 128), jnp.float32),
            pltpu.VMEM((n, 1, ctx_dev), jnp.float32),
            pltpu.VMEM((n, 1, ctx_dev), jnp.float32),
            dma((g,)), dma((g,)),
            dma((n,)), dma((n,)),
            dma, dma,
            dma((n,)), dma((n,)),
            dma((n,)), dma((n,)),
            dma((n,)), dma((n,)),
            dma((n,)), dma((n,)),
            dma((5,)),
        ],
        compiler_params=pltpu.CompilerParams(
            collective_id=0, has_side_effects=True, vmem_limit_bytes=60 * 1024 * 1024
        ),
    )(idx_query, idx_weight, latent_cache.T, idx_keys, q_latent, page_ids)
    return logp.reshape(1, n * ctx_dev), out.reshape(1, H * D_LAT)


def solution(mesh):
    in_specs = (
        P("ctx", "qry"),
        P("ctx", "qry"),
        P("ctx", None),
        P(("ctx", "qry"), None),
        P("ctx", None),
        P(("ctx", "qry"), None),
    )
    out_specs = (P(("ctx", "qry"), None), P(("ctx", "qry"), None))
    return jax.shard_map(
        functools.partial(per_device, mesh.shape["ctx"], mesh.shape["qry"]),
        mesh=mesh, in_specs=in_specs, out_specs=out_specs, check_vma=False,
    )
```

```python
import functools

import jax
import jax.numpy as jnp
from jax import lax
from jax.experimental import pallas as pl
from jax.experimental.pallas import tpu as pltpu
from jax.sharding import PartitionSpec as P

H_IDX = 64
D_IDX = 128
H = 128
D_LAT = 512
D_ROPE = 64
QK_NOPE = 128
PAGE = 64

MESH = pl.DeviceIdType.MESH
LOG2E = 1.4426950408889634
NEG = -1e30


def flip(a, r, n):
    out, bit = 0, 1
    while bit < n:
        x, y = (a // bit) % 2, (r // bit) % 2
        out = out + bit * (x + y - 2 * x * y)
        bit *= 2
    return out


def repeat(lo, hi, body):
    if hi - lo <= 8:
        for i in range(lo, hi):
            body(i)
    else:

        def step(i, carry):
            body(i)
            return carry

        lax.fori_loop(lo, hi, step, 0)


def kernel(
    n, g, group, chunk, ichunk, unroll,
    heads_ref, gains_ref, cache_ref, keys_ref, latent_ref, pages_ref,
    logp_ref, out_ref,
    head_rows, mine_ref, pairs, query_ref, flat_query, wide_gains,
    zed, idx, keys_all, kt, qr, logits, acc, osend, orecv, tsend, trecv, ssend, srecv,
    z_s, z_r, i_s, i_r, k_s, k_r, q_s, q_r, o_s, o_r, t_s, t_r, s_s, s_r, e_s, e_r, loc,
):
    c = lax.axis_index("ctx")
    z = lax.axis_index("qry")
    core = c % 2
    chips = n // 2
    ctx_dev = keys_ref.shape[0]
    width = cache_ref.shape[0]
    half = H // 2
    hb = mine_ref.shape[2]

    barrier = pltpu.get_barrier_semaphore()

    def greet_z(r):
        pl.semaphore_signal(
            barrier, inc=1, device_id=(c, flip(z, r, g)), device_id_type=MESH
        )

    def greet_c(r):
        pl.semaphore_signal(
            barrier, inc=1, device_id=(flip(c, r, n), z), device_id_type=MESH
        )

    repeat(1, g, greet_z)
    repeat(1, n, greet_c)

    own_k = pltpu.make_async_copy(
        cache_ref, kt.at[core, pl.ds(0, width), :], loc.at[1]
    )
    own_k.start()
    own_e = pltpu.make_async_copy(keys_ref, keys_all.at[core], loc.at[5])
    own_e.start()

    for h in range(hb):
        piece = heads_ref[:, h * D_IDX : (h + 1) * D_IDX].astype(jnp.float32)
        for r in range(g):
            head_rows[r, h : h + 1, :] = piece[r : r + 1]
    eye = lax.broadcasted_iota(jnp.int32, (hb, hb), 0) == lax.broadcasted_iota(
        jnp.int32, (hb, hb), 1
    )
    gains = gains_ref[...].astype(jnp.float32)
    for r in range(g):
        mine_ref[r, 0] = head_rows[r].astype(jnp.bfloat16)
        gain = jnp.sum(jnp.where(eye, gains[r : r + 1], 0.0), axis=1, keepdims=True)
        mine_ref[r, 1] = jnp.broadcast_to(gain, (hb, D_IDX)).astype(jnp.bfloat16)

    full = query_ref.shape[3]
    for p in range(half):
        pairs[p : p + 1, :] = latent_ref[:, p * 2 * width : (p + 1) * 2 * width].astype(
            jnp.float32
        )
    topp = pages_ref.shape[1]
    eye = lax.broadcasted_iota(jnp.int32, (topp, topp), 0) == lax.broadcasted_iota(
        jnp.int32, (topp, topp), 1
    )
    ids = jnp.sum(
        jnp.where(eye, pages_ref[...].astype(jnp.float32), 0.0), axis=1, keepdims=True
    )
    spare = 2 * (ctx_dev // PAGE)
    lane = lax.broadcasted_iota(jnp.int32, (topp, 128), 1)
    tail_lane = lax.broadcasted_iota(jnp.int32, (half, 128), 1)
    even = pairs[:, :full]
    odd = pltpu.roll(pairs[:, 2 * width - full :], width, 1)
    for j in range(n // 2):
        page = (lane - (128 - spare) + j * spare).astype(jnp.float32)
        hit = jnp.max(jnp.where(ids == page, 1.0, 0.0), axis=0, keepdims=True)
        flags = jnp.where(hit > 0.5, 0.0, NEG)
        for h, rows in enumerate((even, odd)):
            query_ref[j, h, :, : full - 128] = rows[:, : full - 128].astype(jnp.bfloat16)
            query_ref[j, h, :, full - 128 :] = jnp.where(
                tail_lane < 128 - spare, rows[:, full - 128 :], flags
            ).astype(jnp.bfloat16)

    def z_copy(r):
        peer = flip(z, r, g)
        return pltpu.make_async_remote_copy(
            src_ref=mine_ref.at[peer], dst_ref=zed.at[z],
            send_sem=z_s.at[r], recv_sem=z_r.at[r],
            device_id=(c, peer), device_id_type=MESH,
        )

    def k_copy():
        return pltpu.make_async_remote_copy(
            src_ref=cache_ref, dst_ref=kt.at[core, pl.ds(0, width), :],
            send_sem=k_s, recv_sem=k_r,
            device_id=(flip(c, 1, n), z), device_id_type=MESH,
        )

    def e_copy():
        return pltpu.make_async_remote_copy(
            src_ref=keys_ref, dst_ref=keys_all.at[core],
            send_sem=e_s, recv_sem=e_r,
            device_id=(flip(c, 1, n), z), device_id_type=MESH,
        )

    def c_copy(src, dst, send, recv, r):
        return pltpu.make_async_remote_copy(
            src_ref=src, dst_ref=dst, send_sem=send.at[r], recv_sem=recv.at[r],
            device_id=(flip(c, r, n), z), device_id_type=MESH,
        )

    def q_copy(r):
        peer = flip(c, r, n)
        return c_copy(query_ref.at[peer // 2, peer % 2], qr.at[r], q_s, q_r, r)

    def row_copy(src, dst, send, recv, m):
        return pltpu.make_async_remote_copy(
            src_ref=src, dst_ref=dst, send_sem=send.at[m], recv_sem=recv.at[m],
            device_id=(2 * flip(c // 2, m, chips) + core, z), device_id_type=MESH,
        )

    def i_copy(m):
        return row_copy(zed, idx.at[m], i_s, i_r, m)

    def o_copy(r):
        return c_copy(osend.at[r], orecv.at[r], o_s, o_r, r)

    def t_copy(r):
        return c_copy(tsend.at[r], trecv.at[r], t_s, t_r, r)

    def s_copy(m):
        return row_copy(ssend.at[m], srecv.at[c // 2], s_s, s_r, m)

    pages_dev = ctx_dev // PAGE
    page_row = lax.broadcasted_iota(jnp.int32, (2 * pages_dev, ctx_dev), 0)
    page_col = lax.broadcasted_iota(jnp.int32, (2 * pages_dev, ctx_dev), 1) // PAGE
    for h in range(2):
        kt[h, width:, :] = jnp.where(page_row == page_col + h * pages_dev, 1.0, 0.0).astype(
            jnp.bfloat16
        )

    pl.semaphore_wait(barrier, (g - 1) + (n - 1))

    own_z = pltpu.make_async_copy(mine_ref.at[z], zed.at[z], loc.at[0])
    own_q = pltpu.make_async_copy(query_ref.at[c // 2, core], qr.at[0], loc.at[2])
    own_z.start()
    own_q.start()
    repeat(1, g, lambda r: z_copy(r).start())
    k_copy().start()
    e_copy().start()
    first = max(2, n * 3 // 4)
    repeat(1, first, lambda r: q_copy(r).start())
    own_z.wait()
    repeat(1, g, lambda r: z_copy(r).wait_recv())
    own_i = pltpu.make_async_copy(zed, idx.at[0], loc.at[3])
    own_i.start()
    repeat(1, chips, lambda m: i_copy(m).start())
    repeat(first, n, lambda r: q_copy(r).start())

    def index_rows():
        own_i.wait()
        own_e.wait()
        e_copy().wait_recv()
        repeat(1, chips, lambda m: i_copy(m).wait_recv())
        count = g * hb
        steps = ctx_dev // ichunk

        def lay(r):
            rows = idx[r]
            flat_query[r] = rows[:, 0].reshape(count, D_IDX)
            wide_gains[r] = rows[:, 1].reshape(count, D_IDX).astype(jnp.float32)

        repeat(0, chips, lay)

        def block(s, carry):
            at = pl.ds(pl.multiple_of(s * ichunk, ichunk), ichunk)
            part = pl.ds(pl.multiple_of((s % steps) * ichunk, ichunk), ichunk)
            keys = keys_all[s // steps, part, :]
            for b in range(chips // 4):
                dots = lax.dot_general(
                    flat_query[4 * b : 4 * b + 4].reshape(4 * count, D_IDX), keys,
                    (((1,), (1,)), ((), ())), preferred_element_type=jnp.float32,
                )
                for j in range(4):
                    r = 4 * b + j
                    gain = wide_gains[r]
                    sums = [
                        jnp.sum(
                            jnp.maximum(
                                dots[j * count : (j + 1) * count, t * 128 : (t + 1) * 128], 0.0
                            ) * gain,
                            axis=0, keepdims=True,
                        )
                        for t in range(ichunk // 128)
                    ]
                    ssend[r, :, at] = jnp.concatenate(sums, axis=1)
            return carry

        lax.fori_loop(0, 2 * steps, block, 0)
        repeat(1, chips, lambda m: s_copy(m).start())

    own_s = pltpu.make_async_copy(ssend.at[0], srecv.at[c // 2], loc.at[4])

    own_k.wait()
    own_q.wait()
    k_copy().wait_recv()
    per = ctx_dev // chunk
    scale = ((QK_NOPE + D_ROPE) ** -0.5) * LOG2E
    def rows_of(start, group):
        m_rows = group * half
        for j in range(group):
            r = start + j
            if isinstance(r, int):
                if r > 0:
                    q_copy(r).wait_recv()
            else:

                @pl.when(r > 0)
                def _():
                    q_copy(r).wait_recv()

        def part_one(s, peak):
            keys = pl.ds(pl.multiple_of((s % per) * chunk, chunk), chunk)
            dots = jnp.dot(
                qr[pl.ds(start, group)].reshape(m_rows, qr.shape[2]),
                kt[s // per, :, keys],
                preferred_element_type=jnp.float32,
            ) * scale
            logits[s, :m_rows] = dots
            for t in range(chunk // 128):
                peak = jnp.maximum(peak, dots[:, t * 128 : (t + 1) * 128])
            return peak

        peak = lax.fori_loop(
            0, 2 * per, part_one, jnp.full((m_rows, 128), -jnp.inf, jnp.float32), unroll=unroll
        )
        top = jnp.max(peak, axis=1, keepdims=True)
        acc[:m_rows] = jnp.zeros((m_rows, D_LAT), jnp.float32)

        def part_two(s, total):
            keys = pl.ds(pl.multiple_of((s % per) * chunk, chunk), chunk)
            expo = jnp.exp2(logits[s, :m_rows] - top)
            for t in range(chunk // 128):
                total = total + expo[:, t * 128 : (t + 1) * 128]
            acc[:m_rows] += lax.dot_general(
                expo.astype(jnp.bfloat16), kt[s // per, :D_LAT, keys],
                (((1,), (1,)), ((), ())), preferred_element_type=jnp.float32,
            )
            return total

        total = lax.fori_loop(0, 2 * per, part_two, jnp.zeros((m_rows, 128), jnp.float32), unroll=unroll)
        mass = jnp.sum(total, axis=1, keepdims=True)
        lane = lax.broadcasted_iota(jnp.int32, (m_rows, 128), 1)
        stats = jnp.where(lane == 0, top, mass)
        osend[pl.ds(start, group)] = acc[:m_rows].astype(jnp.bfloat16).reshape(
            group, half, D_LAT
        )
        for j in range(group):
            turned = jnp.transpose(stats[j * half : (j + 1) * half, :])
            tsend[start + j] = jnp.concatenate([turned[:8], turned[:8]], axis=1)
        for j in range(group):
            r = start + j
            if isinstance(r, int):
                if r > 0:
                    t_copy(r).start()
                    o_copy(r).start()
            else:

                @pl.when(r > 0)
                def _():
                    t_copy(r).start()
                    o_copy(r).start()

    plan = [(0, 4), (4, 2), (6, 2), None]
    for piece in plan:
        if piece is None:
            index_rows()
            own_s.start()
        else:
            rows_of(*piece)
    if n > 8:
        repeat(2, n // group, lambda b: rows_of(b * group, group))

    own_s.wait()

    def take_scores(m):
        peer = flip(c // 2, m, chips)
        row_copy(ssend.at[m], srecv.at[peer], s_s, s_r, m).wait_recv()

    repeat(1, chips, take_scores)
    table = srecv[...]
    row_max = jnp.max(table)
    row_total = jnp.sum(jnp.exp(table - row_max), keepdims=True)
    logp_ref[...] = table - (row_max + jnp.log(row_total)) + jnp.log(
        jnp.full((1, 1, 1), n * ctx_dev, jnp.float32)
    )

    def arrive(r):
        t_copy(r).wait_recv()
        o_copy(r).wait_recv()

    repeat(1, n, arrive)
    mixes = []
    for parity in range(2):
        tops, masses = [], []
        for r in range(parity, n, 2):
            stat = tsend[r] if r == 0 else trecv[r]
            col = jnp.transpose(stat)[:half]
            tops.append(col[:, 0:1])
            masses.append(col[:, 1:2])
        best = functools.reduce(jnp.maximum, tops)
        weights = [jnp.exp2(t - best) for t in tops]
        mass = functools.reduce(jnp.add, [w * l for w, l in zip(weights, masses)])
        mixed = jnp.zeros((half, D_LAT), jnp.float32)
        for s, r in enumerate(range(parity, n, 2)):
            value = osend[r] if r == 0 else orecv[r]
            mixed = mixed + value.astype(jnp.float32) * (weights[s] / mass)
        mixes.append(mixed)

    for h in range(2):
        out_ref[:, h * D_LAT : (h + 1) * D_LAT] = jnp.where(
            core == h, mixes[0], mixes[1]
        ).astype(jnp.bfloat16)

    repeat(1, g, lambda r: z_copy(r).wait_send())
    k_copy().wait_send()
    e_copy().wait_send()

    def sent(r):
        q_copy(r).wait_send()
        o_copy(r).wait_send()
        t_copy(r).wait_send()

    repeat(1, n, sent)

    def sent_rows(m):
        i_copy(m).wait_send()
        s_copy(m).wait_send()

    repeat(1, chips, sent_rows)


def per_device(n, g, idx_query, idx_weight, idx_keys, q_latent, latent_cache, page_ids):
    hb = H_IDX // g
    ctx_dev, width = idx_keys.shape[0], latent_cache.shape[1]
    pages_dev = ctx_dev // PAGE
    chips = n // 2
    group, chunk, ichunk, unroll = 4, 1024, 256, True
    full = width + 2 * pages_dev
    half = H // 2
    dma = pltpu.SemaphoreType.DMA
    anywhere = pl.BlockSpec(memory_space=pl.ANY)
    vmem = pl.BlockSpec(memory_space=pltpu.VMEM)
    logp, out = pl.pallas_call(
        functools.partial(kernel, n, g, group, chunk, ichunk, unroll),
        out_shape=(
            jax.ShapeDtypeStruct((chips, 1, 2 * ctx_dev), jnp.float32),
            jax.ShapeDtypeStruct((half, 2 * D_LAT), jnp.bfloat16),
        ),
        in_specs=[vmem, vmem, anywhere, anywhere, vmem, vmem],
        out_specs=(vmem, vmem),
        scratch_shapes=[
            pltpu.VMEM((g, hb, D_IDX), jnp.float32),
            pltpu.VMEM((g, 2, hb, D_IDX), jnp.bfloat16),
            pltpu.VMEM((half, 2 * width), jnp.float32),
            pltpu.VMEM((chips, 2, half, full), jnp.bfloat16),
            pltpu.VMEM((chips, g * hb, D_IDX), jnp.bfloat16),
            pltpu.VMEM((chips, g * hb, D_IDX), jnp.float32),
            pltpu.VMEM((g, 2, hb, D_IDX), jnp.bfloat16),
            pltpu.VMEM((chips, g, 2, hb, D_IDX), jnp.bfloat16),
            pltpu.VMEM((2, ctx_dev, D_IDX), jnp.bfloat16),
            pltpu.VMEM((2, full, ctx_dev), jnp.bfloat16),
            pltpu.VMEM((n, half, full), jnp.bfloat16),
            pltpu.VMEM((2 * ctx_dev // chunk, group * half, chunk), jnp.float32),
            pltpu.VMEM((group * half, D_LAT), jnp.float32),
            pltpu.VMEM((n, half, D_LAT), jnp.bfloat16),
            pltpu.VMEM((n, half, D_LAT), jnp.bfloat16),
            pltpu.VMEM((n, 8, 128), jnp.float32),
            pltpu.VMEM((n, 8, 128), jnp.float32),
            pltpu.VMEM((chips, 1, 2 * ctx_dev), jnp.float32),
            pltpu.VMEM((chips, 1, 2 * ctx_dev), jnp.float32),
            dma((g,)), dma((g,)),
            dma((n,)), dma((n,)),
            dma, dma,
            dma((n,)), dma((n,)),
            dma((n,)), dma((n,)),
            dma((n,)), dma((n,)),
            dma((n,)), dma((n,)),
            dma, dma,
            dma((6,)),
        ],
        compiler_params=pltpu.CompilerParams(
            collective_id=0, has_side_effects=True, vmem_limit_bytes=60 * 1024 * 1024
        ),
    )(idx_query, idx_weight, latent_cache.T, idx_keys, q_latent, page_ids)
    return logp.reshape(1, n * ctx_dev), out.reshape(1, H * D_LAT)


def solution(mesh):
    in_specs = (
        P("ctx", "qry"),
        P("ctx", "qry"),
        P("ctx", None),
        P(("ctx", "qry"), None),
        P("ctx", None),
        P(("ctx", "qry"), None),
    )
    out_specs = (P(("ctx", "qry"), None), P(("ctx", "qry"), None))
    return jax.shard_map(
        functools.partial(per_device, mesh.shape["ctx"], mesh.shape["qry"]),
        mesh=mesh, in_specs=in_specs, out_specs=out_specs, check_vma=False,
    )
```
